32 devices in a mesh: groups: 2 (over y), qring: 4 (over x, core), kvring: 4 (over z), head: 1.
Axes of the slice: x: 2, y: 2, z: 4, core: 2. Of those that a mesh axis runs over, the one named last changes fastest.
Arguments:
- queries: bfloat16 [1536, 4096], P(('groups', 'qring', 'kvring'), 'head'), parts along dimension 0, may hold values from -6 to 6
- keys: bfloat16 [1536, 512], P(('groups', 'qring', 'kvring'), 'head'), parts along dimension 0, may hold values from -6 to 6
- values: bfloat16 [1536, 512], P(('groups', 'qring', 'kvring'), 'head'), parts along dimension 0, may hold values from -6 to 6
- doc_ids: int32 [1536], P('groups'), parts along dimension 0, may hold values from 0 to 15, never falling along the last dimension, each value on 1 to 480 neighbouring positions
- head_mask: int32 [32], P('head'), may hold values 0 or 1
- w_out: bfloat16 [4096, 8192], P('head', 'kvring'), may hold values from -0.5 to 0.5
Outputs:
- mixed: bfloat16 [1536, 8192], P(('groups', 'qring', 'head'), 'kvring'), parts along dimension 0
The draws below stay inside these ranges and needn't reach their ends.
There are 2 independent parts, one for each index of `groups`. The reference program is written for one: setup_inputs(seed, part) draws one part's arguments, and reference() takes and returns one part's arrays. A program takes and returns all parts, laid end to end along the dimension named above; an argument that names none is the same for every part. Nothing has to cross between parts.
All inputs are finite; a program needn't handle non-finite values. No bound on the sum of `head_mask` on one device may be relied on, other than what follows from the above.
Results may differ from the reference program's by a relative error of at most 0.015.
Values may be sent and summed in bfloat16 or wider, within the bound.
A program may use at most 64 MiB of HBM per device.

```python
import math
import jax
import jax.numpy as jnp
import numpy as np
from jax import lax

D = 8192
HEADS = 32
KVH = 4
HD = 128
GROUP = 8
DOCS = 16
SEQ = 768
LONGEST = 480


def draw_queries(key, part):
    base = jnp.clip(1.5 * jax.random.normal(jax.random.fold_in(key, 2), (SEQ, KVH, GROUP, HD), jnp.float32), -6.0, 6.0)
    return base.reshape(SEQ, HEADS * HD).astype(jnp.bfloat16)


def draw_keys(key, part):
    base = jnp.clip(jax.random.normal(jax.random.fold_in(key, 1), (SEQ, KVH, HD), jnp.float32), -6.0, 6.0)
    return base.reshape(SEQ, KVH * HD).astype(jnp.bfloat16)


def plant(drawn, stream_key, low, top_value):
    place = [jax.random.randint(jax.random.fold_in(stream_key, axis), (), 0, length) for axis, length in enumerate(drawn.shape)]
    main_axis = drawn.shape.index(max(drawn.shape))
    next_to = place[:main_axis] + [(place[main_axis] + 1) % drawn.shape[main_axis]] + place[main_axis + 1:]
    return drawn.at[tuple(place)].set(low).at[tuple(next_to)].set(top_value)


def steps_of(rng, extent, pieces, least, high):
    loudness = 1.0
    for axis_at, parts in pieces:
        draws = jax.random.uniform(jax.random.fold_in(jax.random.fold_in(rng, 6), axis_at), (parts,), jnp.float32, least / len(pieces), high / len(pieces))
        loudness = loudness * jnp.repeat(jnp.exp(draws), extent[axis_at] // parts).reshape((-1,) + (1,) * (len(extent) - 1 - axis_at))
    return loudness


def profile(amount, total, most, lean):
    portions = [(1 << 20) // math.isqrt(grade ** lean) + 1 for grade in range(2, amount + 1)]
    spare, holding = total - most - (amount - 1), [1] * (amount - 1)
    while spare > 0:
        free = [i for i in range(amount - 1) if holding[i] < most]
        pool, remaining = sum([portions[i] for i in free]), spare
        for i in free:
            more = min(most - holding[i], max(1, remaining * portions[i] // pool), spare)
            holding[i] = holding[i] + more
            spare = spare - more
    return np.array([most] + holding)


def uneven(key, count, total, most, slope):
    if count == 2:
        one = jax.random.randint(key, (), max(1, total - most), min(most, total - 1) + 1)
        return jnp.stack([one, total - one])
    lengths = jnp.asarray(profile(count, total, most, slope), jnp.int32)
    twos = (count - 1) // 2
    giver, receiver = lengths[1:1 + 2 * twos:2], lengths[2:2 + 2 * twos:2]
    slack = jnp.minimum(giver - 1, most - receiver)
    passed = jax.random.randint(jax.random.fold_in(key, 1), (twos,), 0, 1 << 20) % (slack + 1)
    lengths = lengths.at[1:1 + 2 * twos:2].set(giver - passed).at[2:2 + 2 * twos:2].set(receiver + passed)
    return lengths[jax.random.permutation(jax.random.fold_in(key, 2), count)]


def scatter_about(stream_key, extent, scale, bound, split=(), held_as=jnp.bfloat16):
    array = jax.random.normal(stream_key, extent, jnp.float32) * scale
    if len(split) > 0:
        array = steps_of(stream_key, extent, split, -0.22, 0.18) * array
    return jnp.clip(array, min=-bound, max=bound).astype(held_as)


def setup_inputs(seed: int = 0, part: int = 0) -> dict:
    splits = jax.random.split(jax.random.key(seed), 7)
    part_splits = jax.random.split(jax.random.fold_in(splits[6], part), 7)
    queries = draw_queries(jax.random.fold_in(jax.random.fold_in(splits[6], part), 71), part)
    keys = draw_keys(jax.random.fold_in(jax.random.fold_in(splits[6], part), 71), part)
    values = scatter_about(part_splits[2], (SEQ, KVH * HD), 1.0, 6.0, ((0, 16),))
    doc_ids = jnp.searchsorted(jnp.cumsum(uneven(part_splits[3], DOCS, SEQ, LONGEST, 2)), jnp.arange(SEQ), side="right").astype(jnp.int32)
    head_mask = plant((jax.random.randint(splits[4], (HEADS,), 0, 4) < 3).astype(jnp.int32), jax.random.fold_in(splits[4], 1), 0, 1)
    w_out = scatter_about(splits[5], (HEADS * HD, D), HD ** -0.5, 0.5, ((1, 4),))
    return {"queries": queries, "keys": keys, "values": values, "doc_ids": doc_ids, "head_mask": head_mask, "w_out": w_out}


NEG = -1e+30

def reference(queries, keys, values, doc_ids, head_mask, w_out):
    block_size = math.gcd(SEQ, 256)
    query_all = queries.reshape(SEQ, KVH, GROUP, HD)
    key_all = keys.reshape(SEQ, KVH, HD).astype(jnp.float32)
    value_all = values.reshape(SEQ, KVH, HD).astype(jnp.float32)
    key_pos = jnp.arange(SEQ, dtype=jnp.int32)
    mask_f = head_mask.reshape(KVH, GROUP).astype(jnp.float32)
    scale_factor = 1.0 / math.sqrt(HD)

    def one_block(index):
        start = (index * block_size).astype(jnp.int32)
        query_rows = lax.dynamic_slice_in_dim(query_all, start, block_size, 0).astype(jnp.float32)
        query_doc = lax.dynamic_slice_in_dim(doc_ids, start, block_size, 0)
        query_pos = start + jnp.arange(block_size, dtype=jnp.int32)
        visible = (query_doc[:, None] == doc_ids[None, :]) & (key_pos[None, :] <= query_pos[:, None])
        mask4 = visible[:, None, None, :]
        scores = jnp.einsum('rgec,kgc->rgek', query_rows, key_all) * scale_factor
        scores = jnp.where(mask4, scores, NEG)
        top = lax.optimization_barrier(jnp.max(scores, axis=-1))
        weights = jnp.where(mask4, jnp.exp(scores - top[..., None]), 0.0)
        total = lax.optimization_barrier(jnp.sum(weights, axis=-1))
        rounded = weights.astype(jnp.bfloat16).astype(jnp.float32)
        context = jnp.einsum('rgek,kgc->rgec', rounded, value_all)
        attended = context / total[..., None] * mask_f[None, :, :, None]
        return attended.astype(jnp.bfloat16).reshape(block_size, HEADS * HD)
    blocks = lax.map(one_block, jnp.arange(SEQ // block_size, dtype=jnp.int32))
    attended = blocks.reshape(SEQ, HEADS * HD)
    return jnp.dot(attended, w_out, preferred_element_type=jnp.float32).astype(jnp.bfloat16)
```

```python
import functools
import math

import jax
import jax.numpy as jnp
from jax import lax
from jax.experimental import pallas as pl
from jax.experimental.pallas import tpu as pltpu
from jax.sharding import PartitionSpec as P

HD = 128


NEG = -1e30


def block_rows(total_rows, shard_rows):
    best_size = shard_rows
    for multiple in range(1, total_rows // shard_rows + 1):
        if total_rows // shard_rows % multiple == 0 and multiple * shard_rows <= 256:
            best_size = multiple * shard_rows
    return best_size


def attend_keys(state, visible, queries4, key_rows, value_rows, scale_factor):
    run_max, run_sum, run_out = state
    mask4 = visible[:, None, None, :]
    scores = (
        jnp.einsum("rgec,kgc->rgek", queries4, key_rows, preferred_element_type=jnp.float32)
        * scale_factor
    )
    scores = jnp.where(mask4, scores, NEG)
    new_max = jnp.maximum(run_max, jnp.max(scores, axis=-1))
    weights = jnp.where(mask4, jnp.exp(scores - new_max[..., None]), 0.0)
    shrink = jnp.exp(run_max - new_max)
    run_sum = run_sum * shrink + jnp.sum(weights, axis=-1)
    update = jnp.einsum(
        "rgek,kgc->rgec",
        weights.astype(jnp.bfloat16),
        value_rows,
        preferred_element_type=jnp.float32,
    )
    run_out = run_out * shrink[..., None] + update
    return (new_max, run_sum, run_out)


def fold_piece(
    state, pieces, key_start, queries4, query_doc, query_pos, doc_ids, shard_rows, scale_factor
):
    key_all, value_all = pieces
    total_rows = key_all.shape[0]
    block_size = block_rows(total_rows, shard_rows)

    def one_block(index, carry):
        offset = index * block_size
        key_rows = lax.dynamic_slice_in_dim(key_all, offset, block_size, 0)
        value_rows = lax.dynamic_slice_in_dim(value_all, offset, block_size, 0)
        first = key_start + offset
        key_doc = lax.dynamic_slice_in_dim(doc_ids, first, block_size, 0)
        key_pos = first + jnp.arange(block_size, dtype=jnp.int32)
        visible = (query_doc[:, None] == key_doc[None, :]) & (
            key_pos[None, :] <= query_pos[:, None]
        )
        return attend_keys(carry, visible, queries4, key_rows, value_rows, scale_factor)

    return lax.fori_loop(0, total_rows // block_size, one_block, state)


def per_device(queries, keys, values, doc_ids, head_mask, w_out):
    shard_rows = queries.shape[0]
    kv_local = keys.shape[1] // HD
    q_local = queries.shape[1] // HD
    per_group = q_local // kv_local
    scale_factor = 1.0 / math.sqrt(HD)
    cycle_size = lax.axis_size("kvring")
    cycle_index = lax.axis_index("kvring")
    loop_index = lax.axis_index("qring")
    quarter = cycle_size * shard_rows
    key_rows = keys.reshape(shard_rows, kv_local, HD)
    value_rows = values.reshape(shard_rows, kv_local, HD)
    loop_size = lax.axis_size("qring")
    gathered = lax.all_gather(queries, "qring", axis=0, tiled=True)
    query_total = loop_size * shard_rows
    row_ids = jnp.arange(query_total, dtype=jnp.int32)
    query_pos = row_ids // shard_rows * quarter + cycle_index * shard_rows + row_ids % shard_rows
    queries4 = gathered.reshape(query_total, kv_local, per_group, HD)
    query_doc = jnp.take(doc_ids, query_pos)
    key_base = loop_index * quarter
    initial = (
        jnp.full((query_total, kv_local, per_group), NEG, jnp.float32),
        jnp.zeros((query_total, kv_local, per_group), jnp.float32),
        jnp.zeros((query_total, kv_local, per_group, HD), jnp.float32),
    )
    run_max, run_sum, run_out = fold_piece(
        initial,
        (
            lax.all_gather(key_rows, "kvring", axis=0, tiled=True),
            lax.all_gather(value_rows, "kvring", axis=0, tiled=True),
        ),
        key_base,
        queries4,
        query_doc,
        query_pos,
        doc_ids,
        shard_rows,
        scale_factor,
    )
    top = lax.pmax(run_max, "qring")
    factor = jnp.exp(run_max - top)
    numer, denom = (
        lax.psum_scatter(
            (run_out * factor[..., None]).astype(jnp.bfloat16),
            "qring",
            scatter_dimension=0,
            tiled=True,
        ).astype(jnp.float32),
        lax.psum_scatter(
            (run_sum * factor).astype(jnp.bfloat16), "qring", scatter_dimension=0, tiled=True
        ).astype(jnp.float32),
    )
    mask_f = head_mask.reshape(kv_local, per_group).astype(jnp.float32)
    attended = (
        (numer / denom[..., None] * mask_f[None, :, :, None])
        .astype(jnp.bfloat16)
        .reshape(shard_rows, q_local * HD)
    )
    partial_sum = jnp.dot(
        lax.all_gather(attended, "kvring", axis=0, tiled=True),
        w_out,
        preferred_element_type=jnp.float32,
    )
    return lax.psum_scatter(
        partial_sum.astype(jnp.bfloat16), "head", scatter_dimension=0, tiled=True
    )


LINE = 4
CHUNKS = 8


def fused_kernel(
    rings,
    chunks,
    per_group,
    doc_ref,
    mask_ref,
    q_hbm,
    k_hbm,
    v_hbm,
    w_hbm,
    o_ref,
    q_all,
    k_all,
    v_all,
    w_all,
    attended,
    bias,
    total,
    local_sem,
    w_sem,
    kv_send,
    kv_recv,
    pass_send,
    q_send,
    q_recv,
):
    z = lax.axis_index("kvring")
    q = lax.axis_index("qring")
    shard = q_hbm.shape[0]
    rows = LINE * shard
    seq = k_all.shape[0]
    width = q_hbm.shape[1] // chunks
    per_chunk = width // HD
    scale2 = math.log2(math.e) / math.sqrt(HD)
    order = (2, 1, 3)
    peers = tuple(range(1, rings))

    def other(step):
        return lax.rem(z + step, LINE)

    def ring(step):
        return lax.rem(q + step, rings)

    def far(step):
        gap = z - other(step)
        return (gap == LINE - 1) | (gap == 1 - LINE)

    def near(step):
        return jnp.logical_not(far(step))

    middle = (z == 1) | (z == 2)
    relay_to = 3 * (z - 1)

    def kv_rows(ring_at, line_at):
        return pl.ds(pl.multiple_of((ring_at * LINE + line_at) * shard, 16), shard)

    def q_rows(line_at):
        return pl.ds(pl.multiple_of(line_at * shard, 16), shard)

    def q_cols(c):
        return pl.ds(pl.multiple_of(c * width, 128), width)

    def kv_copies(from_input, line_at, sends, target):
        at = kv_rows(q, line_at)
        slot = q * LINE + line_at
        out = []
        for i, (own, everyone) in enumerate(((k_hbm, k_all), (v_hbm, v_all))):
            out.append(
                pltpu.make_async_remote_copy(
                    src_ref=own if from_input else everyone.at[at],
                    dst_ref=everyone.at[at],
                    send_sem=sends.at[i],
                    recv_sem=kv_recv.at[slot, i],
                    device_id=target,
                    device_id_type=pl.DeviceIdType.MESH,
                )
            )
        return out

    def kv_arrival(ring_at, line_at):
        at = kv_rows(ring_at, line_at)
        slot = ring_at * LINE + line_at
        for i, everyone in enumerate((k_all, v_all)):
            pltpu.make_async_remote_copy(
                src_ref=everyone.at[at],
                dst_ref=everyone.at[at],
                send_sem=kv_send.at[0, i],
                recv_sem=kv_recv.at[slot, i],
                device_id={"kvring": other(1)},
                device_id_type=pl.DeviceIdType.MESH,
            ).wait_recv()

    def q_copy(from_input, line_at, c, step, target):
        place = q_all.at[q_rows(line_at), q_cols(c)]
        return pltpu.make_async_remote_copy(
            src_ref=q_hbm.at[:, q_cols(c)] if from_input else place,
            dst_ref=place,
            send_sem=q_send.at[step, c],
            recv_sem=q_recv.at[line_at, c],
            device_id={"kvring": target},
            device_id_type=pl.DeviceIdType.MESH,
        )

    def w_copy(c):
        at = pl.ds(pl.multiple_of(c * width, 128), width)
        return pltpu.make_async_copy(w_hbm.at[at], w_all.at[at], w_sem.at[c])

    local = [
        pltpu.make_async_copy(q_hbm, q_all.at[q_rows(z)], local_sem.at[0]),
        pltpu.make_async_copy(k_hbm, k_all.at[kv_rows(q, z)], local_sem.at[1]),
        pltpu.make_async_copy(v_hbm, v_all.at[kv_rows(q, z)], local_sem.at[2]),
    ]

    barrier = pltpu.get_barrier_semaphore()
    for step in order:

        @pl.when(near(step))
        def _(step=step):
            pl.semaphore_signal(
                barrier, inc=1, device_id={"kvring": other(step)}, device_id_type=pl.DeviceIdType.MESH
            )

    for step in peers:
        pl.semaphore_signal(
            barrier, inc=1, device_id={"qring": ring(step)}, device_id_type=pl.DeviceIdType.MESH
        )
    for copy in local:
        copy.start()

    @pl.loop(0, chunks)
    def _(c):
        w_copy(c).start()

    @pl.when(middle)
    def _():
        pl.semaphore_wait(barrier, LINE - 1 + len(peers))

    @pl.when(jnp.logical_not(middle))
    def _():
        pl.semaphore_wait(barrier, LINE - 2 + len(peers))

    def send_kv_on(from_input, line_at, place):
        for i, step in enumerate(peers):
            for copy in kv_copies(from_input, line_at, pass_send.at[place, i], {"qring": ring(step)}):
                copy.start()

    def send_q(first, last):
        @pl.loop(first, last)
        def _(c):
            for step in order:

                @pl.when(near(step))
                def _(step=step):
                    q_copy(True, z, c, step, other(step)).start()

    for step in order:

        @pl.when(near(step))
        def _(step=step):
            for copy in kv_copies(True, z, kv_send.at[step], {"kvring": other(step)}):
                copy.start()

    send_kv_on(True, z, 0)
    quota = chunks // LINE
    send_q(0, quota)
    for i, step in enumerate(order):
        kv_arrival(q, other(step))
        if step == 2:

            @pl.when(middle)
            def _():
                for copy in kv_copies(False, other(2), kv_send.at[0], {"kvring": relay_to}):
                    copy.start()

        send_kv_on(False, other(step), step)
        send_q((i + 1) * quota, (i + 2) * quota)

    def q_arrival(step, c):
        q_copy(False, other(step), c, 0, other(1)).wait_recv()

    def relay(c):
        q_arrival(2, c)

        @pl.when(middle)
        def _():
            q_copy(False, other(2), c, 0, relay_to).start()

    relay(0)

    row_at = q * rows + lax.broadcasted_iota(jnp.int32, (rows, seq), 0)
    key_at = lax.broadcasted_iota(jnp.int32, (rows, seq), 1)
    key_doc = jnp.broadcast_to(doc_ref[...], (rows, seq))
    row_doc = jnp.sum(jnp.where(row_at == key_at, key_doc, 0), axis=1, keepdims=True)
    bias[...] = jnp.where((key_doc == row_doc) & (key_at <= row_at), 0.0, NEG)
    total[...] = jnp.zeros_like(total)

    for copy in local:
        copy.wait()
    for step in peers:
        for line_at in range(LINE):
            kv_arrival(ring(step), line_at)

    @pl.loop(0, chunks)
    def _(c):
        for step in (1, 3):
            q_arrival(step, c)
        kv_head = c * per_chunk // per_group
        kv_cols = pl.ds(pl.multiple_of(kv_head * HD, 128), HD)
        for e in range(per_chunk):
            head = c * per_chunk + e
            queries = q_all[:, pl.ds(pl.multiple_of(head * HD, 128), HD)]
            scores = lax.dot_general(
                queries,
                k_all[:, kv_cols],
                (((1,), (1,)), ((), ())),
                preferred_element_type=jnp.float32,
            )
            scores = scores * scale2 + bias[...]
            top = jnp.max(scores, axis=-1, keepdims=True)
            weights = jnp.exp2(scores - top)
            denom = jnp.sum(weights, axis=-1, keepdims=True)
            context = jnp.dot(
                weights.astype(jnp.bfloat16), v_all[:, kv_cols], preferred_element_type=jnp.float32
            )
            keep = mask_ref[head].astype(jnp.float32)
            attended[:, e * HD : (e + 1) * HD] = (context / denom * keep).astype(jnp.bfloat16)

        @pl.when(c + 1 < chunks)
        def _():
            relay(c + 1)

        w_copy(c).wait()
        total[...] += jnp.dot(
            attended[...],
            w_all[pl.ds(pl.multiple_of(c * width, 128), width), :],
            preferred_element_type=jnp.float32,
        )

    o_ref[...] = total[...].astype(jnp.bfloat16)

    for step in order:

        @pl.when(near(step))
        def _(step=step):
            for copy in kv_copies(True, z, kv_send.at[step], {"kvring": other(step)}):
                copy.wait_send()

            @pl.loop(0, chunks)
            def _(c):
                q_copy(True, z, c, step, other(step)).wait_send()

    @pl.when(middle)
    def _():
        for copy in kv_copies(False, other(2), kv_send.at[0], {"kvring": relay_to}):
            copy.wait_send()

        @pl.loop(0, chunks)
        def _(c):
            q_copy(False, other(2), c, 0, relay_to).wait_send()

    for place in range(LINE):
        for i, step in enumerate(peers):
            for copy in kv_copies(place == 0, other(place), pass_send.at[place, i], {"qring": ring(step)}):
                copy.wait_send()


def fused_device(queries, keys, values, doc_ids, head_mask, w_out):
    shard_rows = queries.shape[0]
    rings = lax.axis_size("qring")
    seq = doc_ids.shape[0]
    rows = LINE * shard_rows
    columns = w_out.shape[1]
    width = queries.shape[1] // CHUNKS
    per_group = queries.shape[1] // keys.shape[1]
    vmem = pl.BlockSpec(memory_space=pltpu.VMEM)
    anywhere = pl.BlockSpec(memory_space=pl.ANY)
    dma = pltpu.SemaphoreType.DMA
    return pl.pallas_call(
        functools.partial(fused_kernel, rings, CHUNKS, per_group),
        out_shape=jax.ShapeDtypeStruct((rows, columns), jnp.bfloat16),
        in_specs=[vmem, pl.BlockSpec(memory_space=pltpu.SMEM), anywhere, anywhere, anywhere, anywhere],
        out_specs=vmem,
        scratch_shapes=[
            pltpu.VMEM((rows, queries.shape[1]), jnp.bfloat16),
            pltpu.VMEM((seq, keys.shape[1]), jnp.bfloat16),
            pltpu.VMEM((seq, keys.shape[1]), jnp.bfloat16),
            pltpu.VMEM(w_out.shape, jnp.bfloat16),
            pltpu.VMEM((rows, width), jnp.bfloat16),
            pltpu.VMEM((rows, seq), jnp.float32),
            pltpu.VMEM((rows, columns), jnp.float32),
            dma((3,)),
            dma((CHUNKS,)),
            dma((LINE, 2)),
            dma((rings * LINE, 2)),
            dma((LINE, rings - 1, 2)),
            dma((LINE, CHUNKS)),
            dma((LINE, CHUNKS)),
        ],
        compiler_params=pltpu.CompilerParams(
            collective_id=0, has_side_effects=True, vmem_limit_bytes=48 * 1024 * 1024
        ),
    )(doc_ids.reshape(1, seq), head_mask, queries, keys, values, w_out)


def solution(mesh):
    small = mesh.shape["kvring"] == LINE and mesh.shape["head"] == 1
    placed = (
        P(("groups", "qring", "kvring"), "head"),
        P(("groups", "qring", "kvring"), "head"),
        P(("groups", "qring", "kvring"), "head"),
        P("groups"),
        P("head"),
        P("head", "kvring"),
    )
    return jax.shard_map(
        fused_device if small else per_device,
        mesh=mesh,
        in_specs=placed,
        out_specs=P(("groups", "qring", "head"), "kvring"),
        check_vma=False,
    )
```

```python
import functools
import math

import jax
import jax.numpy as jnp
from jax import lax
from jax.experimental import pallas as pl
from jax.experimental.pallas import tpu as pltpu
from jax.sharding import PartitionSpec as P

HD = 128


NEG = -1e30


def block_rows(total_rows, shard_rows):
    best_size = shard_rows
    for multiple in range(1, total_rows // shard_rows + 1):
        if total_rows // shard_rows % multiple == 0 and multiple * shard_rows <= 256:
            best_size = multiple * shard_rows
    return best_size


def attend_keys(state, visible, queries4, key_rows, value_rows, scale_factor):
    run_max, run_sum, run_out = state
    mask4 = visible[:, None, None, :]
    scores = (
        jnp.einsum("rgec,kgc->rgek", queries4, key_rows, preferred_element_type=jnp.float32)
        * scale_factor
    )
    scores = jnp.where(mask4, scores, NEG)
    new_max = jnp.maximum(run_max, jnp.max(scores, axis=-1))
    weights = jnp.where(mask4, jnp.exp(scores - new_max[..., None]), 0.0)
    shrink = jnp.exp(run_max - new_max)
    run_sum = run_sum * shrink + jnp.sum(weights, axis=-1)
    update = jnp.einsum(
        "rgek,kgc->rgec",
        weights.astype(jnp.bfloat16),
        value_rows,
        preferred_element_type=jnp.float32,
    )
    run_out = run_out * shrink[..., None] + update
    return (new_max, run_sum, run_out)


def fold_piece(
    state, pieces, key_start, queries4, query_doc, query_pos, doc_ids, shard_rows, scale_factor
):
    key_all, value_all = pieces
    total_rows = key_all.shape[0]
    block_size = block_rows(total_rows, shard_rows)

    def one_block(index, carry):
        offset = index * block_size
        key_rows = lax.dynamic_slice_in_dim(key_all, offset, block_size, 0)
        value_rows = lax.dynamic_slice_in_dim(value_all, offset, block_size, 0)
        first = key_start + offset
        key_doc = lax.dynamic_slice_in_dim(doc_ids, first, block_size, 0)
        key_pos = first + jnp.arange(block_size, dtype=jnp.int32)
        visible = (query_doc[:, None] == key_doc[None, :]) & (
            key_pos[None, :] <= query_pos[:, None]
        )
        return attend_keys(carry, visible, queries4, key_rows, value_rows, scale_factor)

    return lax.fori_loop(0, total_rows // block_size, one_block, state)


def per_device(queries, keys, values, doc_ids, head_mask, w_out):
    shard_rows = queries.shape[0]
    kv_local = keys.shape[1] // HD
    q_local = queries.shape[1] // HD
    per_group = q_local // kv_local
    scale_factor = 1.0 / math.sqrt(HD)
    cycle_size = lax.axis_size("kvring")
    cycle_index = lax.axis_index("kvring")
    loop_index = lax.axis_index("qring")
    quarter = cycle_size * shard_rows
    key_rows = keys.reshape(shard_rows, kv_local, HD)
    value_rows = values.reshape(shard_rows, kv_local, HD)
    loop_size = lax.axis_size("qring")
    gathered = lax.all_gather(queries, "qring", axis=0, tiled=True)
    query_total = loop_size * shard_rows
    row_ids = jnp.arange(query_total, dtype=jnp.int32)
    query_pos = row_ids // shard_rows * quarter + cycle_index * shard_rows + row_ids % shard_rows
    queries4 = gathered.reshape(query_total, kv_local, per_group, HD)
    query_doc = jnp.take(doc_ids, query_pos)
    key_base = loop_index * quarter
    initial = (
        jnp.full((query_total, kv_local, per_group), NEG, jnp.float32),
        jnp.zeros((query_total, kv_local, per_group), jnp.float32),
        jnp.zeros((query_total, kv_local, per_group, HD), jnp.float32),
    )
    run_max, run_sum, run_out = fold_piece(
        initial,
        (
            lax.all_gather(key_rows, "kvring", axis=0, tiled=True),
            lax.all_gather(value_rows, "kvring", axis=0, tiled=True),
        ),
        key_base,
        queries4,
        query_doc,
        query_pos,
        doc_ids,
        shard_rows,
        scale_factor,
    )
    top = lax.pmax(run_max, "qring")
    factor = jnp.exp(run_max - top)
    numer, denom = (
        lax.psum_scatter(
            (run_out * factor[..., None]).astype(jnp.bfloat16),
            "qring",
            scatter_dimension=0,
            tiled=True,
        ).astype(jnp.float32),
        lax.psum_scatter(
            (run_sum * factor).astype(jnp.bfloat16), "qring", scatter_dimension=0, tiled=True
        ).astype(jnp.float32),
    )
    mask_f = head_mask.reshape(kv_local, per_group).astype(jnp.float32)
    attended = (
        (numer / denom[..., None] * mask_f[None, :, :, None])
        .astype(jnp.bfloat16)
        .reshape(shard_rows, q_local * HD)
    )
    partial_sum = jnp.dot(
        lax.all_gather(attended, "kvring", axis=0, tiled=True),
        w_out,
        preferred_element_type=jnp.float32,
    )
    return lax.psum_scatter(
        partial_sum.astype(jnp.bfloat16), "head", scatter_dimension=0, tiled=True
    )


LINE = 4
CHUNKS = 8
RAW = 3
RINGS = 4
VMEM_LIMIT = 66200000


def fused_kernel(
    chunks,
    per_group,
    doc_hbm,
    mask_hbm,
    q_hbm,
    k_hbm,
    v_hbm,
    w_hbm,
    o_ref,
    doc_row,
    mask_ref,
    q_all,
    k_all,
    v_all,
    w_all,
    attended,
    bias,
    total,
    local_sem,
    w_sem,
    kv_send,
    kv_recv,
    pass_send,
    mate_send,
    q_send,
    q_recv,
):
    z = lax.axis_index("kvring")
    q = lax.axis_index("qring")
    shard = q_hbm.shape[0]
    rows = LINE * shard
    seq = k_all.shape[0]
    width = q_hbm.shape[1] // chunks
    per_chunk = width // HD
    scale2 = math.log2(math.e) / math.sqrt(HD)
    order = (2, 1, 3)
    across = lax.rem(q + 2, RINGS)
    mate = q + 1 - 2 * lax.rem(q, 2)
    across_of_mate = lax.rem(mate + 2, RINGS)

    def other(step):
        return lax.rem(z + step, LINE)

    def far(step):
        gap = z - other(step)
        return (gap == LINE - 1) | (gap == 1 - LINE)

    def near(step):
        return jnp.logical_not(far(step))

    middle = (z == 1) | (z == 2)
    relay_to = 3 * (z - 1)

    def kv_rows(ring_at, line_at):
        return pl.ds(pl.multiple_of((ring_at * LINE + line_at) * shard, 16), shard)

    def q_rows(line_at):
        return pl.ds(pl.multiple_of(line_at * shard, 16), shard)

    def q_cols(c):
        return pl.ds(pl.multiple_of(c * width, 128), width)

    def kv_copies(from_input, line_at, sends, target, ring_at=q):
        at = kv_rows(ring_at, line_at)
        slot = ring_at * LINE + line_at
        out = []
        for i, (own, everyone) in enumerate(((k_hbm, k_all), (v_hbm, v_all))):
            out.append(
                pltpu.make_async_remote_copy(
                    src_ref=own if from_input else everyone.at[at],
                    dst_ref=everyone.at[at],
                    send_sem=sends.at[i],
                    recv_sem=kv_recv.at[slot, i],
                    device_id=target,
                    device_id_type=pl.DeviceIdType.MESH,
                )
            )
        return out

    def kv_arrival(ring_at, line_at):
        at = kv_rows(ring_at, line_at)
        slot = ring_at * LINE + line_at
        for i, everyone in enumerate((k_all, v_all)):
            pltpu.make_async_remote_copy(
                src_ref=everyone.at[at],
                dst_ref=everyone.at[at],
                send_sem=kv_send.at[0, i],
                recv_sem=kv_recv.at[slot, i],
                device_id={"kvring": other(1)},
                device_id_type=pl.DeviceIdType.MESH,
            ).wait_recv()

    def q_copy(from_input, line_at, c, step, target):
        place = q_all.at[q_rows(line_at), q_cols(c)]
        return pltpu.make_async_remote_copy(
            src_ref=q_hbm.at[:, q_cols(c)] if from_input else place,
            dst_ref=place,
            send_sem=q_send.at[step, c],
            recv_sem=q_recv.at[line_at, c],
            device_id={"kvring": target},
            device_id_type=pl.DeviceIdType.MESH,
        )

    def w_copy(c):
        at = pl.ds(pl.multiple_of(c * width, 128), width)
        return pltpu.make_async_copy(w_hbm.at[at], w_all.at[at], w_sem.at[c])

    local = [
        pltpu.make_async_copy(q_hbm, q_all.at[q_rows(z)], local_sem.at[0]),
        pltpu.make_async_copy(k_hbm, k_all.at[kv_rows(q, z)], local_sem.at[1]),
        pltpu.make_async_copy(v_hbm, v_all.at[kv_rows(q, z)], local_sem.at[2]),
    ]

    doc_copy = pltpu.make_async_copy(doc_hbm, doc_row, local_sem.at[3])
    mask_copy = pltpu.make_async_copy(mask_hbm, mask_ref, local_sem.at[4])

    barrier = pltpu.get_barrier_semaphore()
    for step in order:

        @pl.when(near(step))
        def _(step=step):
            pl.semaphore_signal(
                barrier, inc=1, device_id={"kvring": other(step)}, device_id_type=pl.DeviceIdType.MESH
            )

    for ring_at in (across, mate):
        pl.semaphore_signal(
            barrier, inc=1, device_id={"qring": ring_at}, device_id_type=pl.DeviceIdType.MESH
        )
    for copy in (doc_copy, mask_copy, *local):
        copy.start()

    @pl.loop(0, chunks)
    def _(c):
        w_copy(c).start()

    @pl.when(middle)
    def _():
        pl.semaphore_wait(barrier, LINE + 1)

    @pl.when(jnp.logical_not(middle))
    def _():
        pl.semaphore_wait(barrier, LINE)

    def send_kv_on(from_input, line_at, place):
        for i, ring_at in enumerate((across, mate)):
            for copy in kv_copies(from_input, line_at, pass_send.at[place, i], {"qring": ring_at}):
                copy.start()

    def kv_to_mate(line_at, place):
        return kv_copies(False, line_at, mate_send.at[place], {"qring": mate}, across)

    def send_across_on(line_at, place):
        kv_arrival(across, line_at)
        for copy in kv_to_mate(line_at, place):
            copy.start()

    def send_q(from_input, c):
        for step in order:

            @pl.when(near(step))
            def _(step=step):
                q_copy(from_input, z, c, step, other(step)).start()

    def q_arrival(step, c):
        q_copy(False, other(step), c, 0, other(1)).wait_recv()

    def relay(c):
        q_arrival(2, c)

        @pl.when(middle)
        def _():
            q_copy(False, other(2), c, 0, relay_to).start()

    for step in order:

        @pl.when(near(step))
        def _(step=step):
            for copy in kv_copies(True, z, kv_send.at[step], {"kvring": other(step)}):
                copy.start()

    send_kv_on(True, z, 0)
    send_q(True, 0)
    behind = (0,) + order
    for i, step in enumerate(order):
        kv_arrival(q, other(step))
        if step == 2:

            @pl.when(middle)
            def _():
                for copy in kv_copies(False, other(2), kv_send.at[0], {"kvring": relay_to}):
                    copy.start()

        send_kv_on(False, other(step), step)
        if i + 1 < RAW:
            send_q(True, i + 1)
        send_across_on(other(behind[i]), behind[i])

    doc_copy.wait()
    row_at = q * rows + lax.broadcasted_iota(jnp.int32, (rows, seq), 0)
    key_at = lax.broadcasted_iota(jnp.int32, (rows, seq), 1)
    key_doc = jnp.broadcast_to(doc_row[...].reshape(1, seq), (rows, seq))
    row_doc = jnp.sum(jnp.where(row_at == key_at, key_doc, 0), axis=1, keepdims=True)
    bias[...] = jnp.where((key_doc == row_doc) & (key_at <= row_at), 0.0, NEG)
    send_across_on(other(3), 3)
    relay(0)
    mask_copy.wait()
    for copy in local:
        copy.wait()
    for place in (0,) + order:
        kv_arrival(mate, other(place))
    for place in (0,) + order:
        kv_arrival(across_of_mate, other(place))

    def attend(queries, hidden, kv_head):
        kv_cols = pl.ds(pl.multiple_of(kv_head * HD, 128), HD)
        scores = lax.dot_general(
            queries, k_all[:, kv_cols], (((1,), (1,)), ((), ())), preferred_element_type=jnp.float32
        )
        parts = queries.shape[0] // hidden.shape[0]
        scores = (scores * scale2).reshape(parts, hidden.shape[0], seq) + hidden[None]
        scores = scores.reshape(queries.shape[0], seq)
        top = jnp.max(scores, axis=-1, keepdims=True)
        weights = jnp.exp2(scores - top)
        denom = jnp.sum(weights, axis=-1, keepdims=True)
        context = jnp.dot(
            weights.astype(jnp.bfloat16), v_all[:, kv_cols], preferred_element_type=jnp.float32
        )
        return context / denom

    def head_cols(head):
        return pl.ds(pl.multiple_of(head * HD, 128), HD)

    @pl.loop(RAW, chunks)
    def _(c):
        heads = [c * per_chunk + e for e in range(per_chunk)]
        stacked = jnp.concatenate([q_all[q_rows(z), head_cols(head)] for head in heads], axis=0)
        result = attend(stacked, bias[q_rows(z), :], c * per_chunk // per_group)
        for e, head in enumerate(heads):
            keep = mask_ref[head].astype(jnp.float32)
            piece = result[e * shard : (e + 1) * shard] * keep
            q_all[q_rows(z), head_cols(head)] = piece.astype(jnp.bfloat16)

        @pl.when(c > RAW)
        def _():
            send_q(False, c - 1)

        @pl.when(c - RAW + 1 < RAW)
        def _():
            relay(c - RAW + 1)

    def weights_of(c):
        w_copy(c).wait()
        return w_all[pl.ds(pl.multiple_of(c * width, 128), width), :]

    @pl.loop(0, RAW)
    def _(c):
        @pl.when(c == 0)
        def _():
            send_q(False, chunks - 1)

        for step in (1, 3):
            q_arrival(step, c)
        for e in range(per_chunk):
            head = c * per_chunk + e
            result = attend(q_all[:, head_cols(head)], bias[...], c * per_chunk // per_group)
            keep = mask_ref[head].astype(jnp.float32)
            attended[:, e * HD : (e + 1) * HD] = (result * keep).astype(jnp.bfloat16)
        relay(c + RAW)
        fresh = jnp.dot(attended[...], weights_of(c), preferred_element_type=jnp.float32)

        @pl.when(c == 0)
        def _():
            total[...] = fresh

        @pl.when(c > 0)
        def _():
            total[...] += fresh

    @pl.loop(RAW, chunks)
    def _(c):
        @pl.when(c + RAW < chunks)
        def _():
            relay(c + RAW)

        for step in (1, 3):
            q_arrival(step, c)
        total[...] += jnp.dot(
            q_all[:, q_cols(c)], weights_of(c), preferred_element_type=jnp.float32
        )

    o_ref[...] = total[...].astype(jnp.bfloat16)

    for step in order:

        @pl.when(near(step))
        def _(step=step):
            for copy in kv_copies(True, z, kv_send.at[step], {"kvring": other(step)}):
                copy.wait_send()

            @pl.loop(0, chunks)
            def _(c):
                q_copy(True, z, c, step, other(step)).wait_send()

    @pl.when(middle)
    def _():
        for copy in kv_copies(False, other(2), kv_send.at[0], {"kvring": relay_to}):
            copy.wait_send()

        @pl.loop(0, chunks)
        def _(c):
            q_copy(False, other(2), c, 0, relay_to).wait_send()

    for place in range(LINE):
        for i, ring_at in enumerate((across, mate)):
            for copy in kv_copies(place == 0, other(place), pass_send.at[place, i], {"qring": ring_at}):
                copy.wait_send()
        for copy in kv_to_mate(other(place), place):
            copy.wait_send()


def fused_device(queries, keys, values, doc_ids, head_mask, w_out):
    shard_rows = queries.shape[0]
    seq = doc_ids.shape[0]
    rows = LINE * shard_rows
    columns = w_out.shape[1]
    width = queries.shape[1] // CHUNKS
    per_group = queries.shape[1] // keys.shape[1]
    vmem = pl.BlockSpec(memory_space=pltpu.VMEM)
    anywhere = pl.BlockSpec(memory_space=pl.ANY)
    dma = pltpu.SemaphoreType.DMA
    return pl.pallas_call(
        functools.partial(fused_kernel, CHUNKS, per_group),
        out_shape=jax.ShapeDtypeStruct((rows, columns), jnp.bfloat16),
        in_specs=[anywhere] * 6,
        out_specs=vmem,
        scratch_shapes=[
            pltpu.VMEM((seq,), jnp.int32),
            pltpu.SMEM(head_mask.shape, jnp.int32),
            pltpu.VMEM((rows, queries.shape[1]), jnp.bfloat16),
            pltpu.VMEM((seq, keys.shape[1]), jnp.bfloat16),
            pltpu.VMEM((seq, keys.shape[1]), jnp.bfloat16),
            pltpu.VMEM(w_out.shape, jnp.bfloat16),
            pltpu.VMEM((rows, width), jnp.bfloat16),
            pltpu.VMEM((rows, seq), jnp.float32),
            pltpu.VMEM((rows, columns), jnp.float32),
            dma((5,)),
            dma((CHUNKS,)),
            dma((LINE, 2)),
            dma((RINGS * LINE, 2)),
            dma((LINE, 2, 2)),
            dma((LINE, 2)),
            dma((LINE, CHUNKS)),
            dma((LINE, CHUNKS)),
        ],
        compiler_params=pltpu.CompilerParams(
            collective_id=0, has_side_effects=True, vmem_limit_bytes=VMEM_LIMIT
        ),
    )(doc_ids, head_mask, queries, keys, values, w_out)


def solution(mesh):
    sizes = (mesh.shape["qring"], mesh.shape["kvring"], mesh.shape["head"])
    small = sizes == (RINGS, LINE, 1)
    placed = (
        P(("groups", "qring", "kvring"), "head"),
        P(("groups", "qring", "kvring"), "head"),
        P(("groups", "qring", "kvring"), "head"),
        P("groups"),
        P("head"),
        P("head", "kvring"),
    )
    return jax.shard_map(
        fused_device if small else per_device,
        mesh=mesh,
        in_specs=placed,
        out_specs=P(("groups", "qring", "head"), "kvring"),
        check_vma=False,
    )
```
